32 devices in a mesh: section: 2 (over x), seq: 16 (over z, y, core).
Axes of the slice: x: 2, y: 2, z: 4, core: 2. Of those that a mesh axis runs over, the one named last changes fastest.
Arguments:
- section_input: bfloat16 [2, 2, 2048, 2048], P('section', None, 'seq'), may hold values from -6 to 6
- out_grad: bfloat16 [2, 2048, 2048], P(None, 'seq'), may hold values from -6 to 6
- norm_gain: float32 [2, 2048], P('section'), may hold values from 0.1 to 1.9
- query_weight: bfloat16 [2, 2048, 1024], P('section', 'seq'), may hold values from -0.125 to 0.125
- output_weight: bfloat16 [2, 1024, 2048], P('section', 'seq'), may hold values from -0.1875 to 0.1875
- header_keys: bfloat16 [2, 2, 64, 256], P('section', None, 'seq'), may hold values from -6 to 6
- header_values: bfloat16 [2, 2, 64, 256], P('section', None, 'seq'), may hold values from -6 to 6
- header_pos: int32 [2, 64], replicated, may hold values from 0 to 2047
- segment_ids: int32 [2, 2048], P(None, 'seq'), may hold values from 0 to 7, never falling along the last dimension, each value on 1 to 512 neighbouring positions
Outputs:
- grad_input: bfloat16 [2, 2, 2048, 2048], P('section', None, 'seq')
- header_key_gradient: float32 [2, 2, 64, 256], P('section', None, 'seq')
- header_value_gradient: float32 [2, 2, 64, 256], P('section', None, 'seq')
The draws below stay inside these ranges and needn't reach their ends.
Inputs may be any that keep to these rules, and one draw needn't show every extreme that they name: `segment_ids`: ids never fall along a sheet's cells; every id occurs, and no id covers more than 512 cells.
All inputs are finite; a program needn't handle non-finite values.
Results may differ from the reference program's by a relative error of at most 0.0085.
Values may be sent and summed in bfloat16 or wider, within the bound.
A program may use at most 64 MiB of HBM per device.

```python
import math
import jax
import jax.numpy as jnp
import numpy as np
from jax import lax

D = 2048
HQ = 16
KEY_HEADS = 4
HEAD_WIDTH = 64
HPS = 8
MB = 2
QUERY_PER_KV = 4
QW = 1024
KVW = 256
CELLS = 2048
NH = 64
NSEG = 8
N_SECTION = 2


def with_ends(drawn, own_key, low, top_value):
    index_at = [jax.random.randint(jax.random.fold_in(own_key, axis), (), 0, length) for axis, length in enumerate(drawn.shape)]
    widest = drawn.shape.index(max(drawn.shape))
    neighbour = index_at[:widest] + [(index_at[widest] + 1) % drawn.shape[widest]] + index_at[widest + 1:]
    return drawn.at[tuple(index_at)].set(low).at[tuple(neighbour)].set(top_value)


def block_scale(key, extent, split, smallest, largest):
    gain = 1.0
    for dim, blocks in split:
        draws = jax.random.uniform(jax.random.fold_in(jax.random.fold_in(key, 6), dim), (blocks,), jnp.float32, smallest / len(split), largest / len(split))
        gain = gain * jnp.repeat(jnp.exp(draws), extent[dim] // blocks).reshape((-1,) + (1,) * (len(extent) - 1 - dim))
    return gain


def split_up(amount, total, most, slope):
    weights = [(1 << 20) // math.isqrt(rank ** slope) + 1 for rank in range(2, amount + 1)]
    spare, given = total - most - (amount - 1), [1] * (amount - 1)
    while spare > 0:
        movable = [i for i in range(amount - 1) if given[i] < most]
        whole, budget = sum([weights[i] for i in movable]), spare
        for i in movable:
            extra = min(most - given[i], max(1, budget * weights[i] // whole), spare)
            given[i] = given[i] + extra
            spare = spare - extra
    return np.array([most] + given)


def ragged(rng, number_of, total, limit, skew):
    if number_of == 2:
        one = jax.random.randint(rng, (), max(1, total - limit), min(limit, total - 1) + 1)
        return jnp.stack([one, total - one])
    lengths = jnp.asarray(split_up(number_of, total, limit, skew), jnp.int32)
    couples = (number_of - 1) // 2
    giver, taker = lengths[1:1 + 2 * couples:2], lengths[2:2 + 2 * couples:2]
    slack = jnp.minimum(giver - 1, limit - taker)
    moved = jax.random.randint(jax.random.fold_in(rng, 1), (couples,), 0, 1 << 20) % (slack + 1)
    lengths = lengths.at[1:1 + 2 * couples:2].set(giver - moved).at[2:2 + 2 * couples:2].set(taker + moved)
    return lengths[jax.random.permutation(jax.random.fold_in(rng, 2), number_of)]


def gaussian(rng, dims, scale, limit, cuts=(), held_as=jnp.bfloat16):
    level = block_scale(rng, dims, cuts, -0.22, 0.18) if cuts else 1.0
    result = jax.random.normal(rng, dims, jnp.float32) * scale * level
    return jnp.minimum(jnp.maximum(result, -limit), limit).astype(held_as)


def setup_inputs(seed: int = 0) -> dict:
    keys = jax.random.split(jax.random.key(seed), 10)
    return {
        "section_input": gaussian(keys[0], (N_SECTION, MB, CELLS, D), 1.0, 6.0, ((0, 2), (2, 16))),
        "out_grad": gaussian(keys[1], (MB, CELLS, D), 1.0, 6.0, ((1, 16),)),
        "norm_gain": jnp.clip(1.0 + 0.18 * jax.random.normal(keys[2], (N_SECTION, D), jnp.float32), 0.1, 1.9),
        "query_weight": gaussian(keys[3], (N_SECTION, D, QW), D ** -0.5, 0.125, ((0, 2), (1, 16))),
        "output_weight": gaussian(keys[4], (N_SECTION, QW, D), QW ** -0.5, 0.1875, ((0, 2), (1, 16))),
        "header_keys": gaussian(keys[5], (N_SECTION, MB, NH, KVW), 1.0, 6.0, ((0, 2), (2, 16))),
        "header_values": gaussian(keys[6], (N_SECTION, MB, NH, KVW), 1.0, 6.0, ((0, 2), (2, 16))),
        "header_pos": with_ends(jax.random.randint(keys[7], (MB, NH), 0, CELLS), jax.random.fold_in(keys[7], 1), 0, CELLS - 1).astype(jnp.int32),
        "segment_ids": jax.vmap(lambda own: jnp.searchsorted(jnp.cumsum(ragged(own, NSEG, CELLS, 2 * CELLS // NSEG, 2)), jnp.arange(CELLS), side="right"))(jax.random.split(keys[8], MB)).reshape((MB, CELLS)).astype(jnp.int32),
    }


EPSILON = 1e-05
ROPE_BASE = 500000.0

def rope_tables(positions, half_width):
    freq_index = jnp.arange(half_width, dtype=jnp.float32)
    inverse = jnp.exp(freq_index * (-2.0 * math.log(ROPE_BASE) / (2 * half_width)))
    angles = positions.astype(jnp.float32)[..., None] * inverse
    return (jnp.cos(angles), jnp.sin(angles))

def apply_rotary(vectors, cosine, sine_part):
    half_width = vectors.shape[-1] // 2
    first_half = vectors[..., :half_width]
    second = vectors[..., half_width:]
    cos_wide = cosine[..., None, :]
    sin_wide = sine_part[..., None, :]
    return jnp.concatenate([first_half * cos_wide - second * sin_wide, second * cos_wide + first_half * sin_wide], axis=-1)

def layer_backward(section_rows, norm_scale, query_full, output_full, unrotated_keys, plain_values, header_positions, segments, grad_output):
    cell_number = section_rows.shape[0]
    score_scale = HEAD_WIDTH ** (-0.5)
    widened = section_rows.astype(jnp.float32)
    inv_rms = lax.rsqrt(lax.optimization_barrier(jnp.mean(widened * widened, axis=-1, keepdims=True)) + EPSILON)
    normed = (widened * inv_rms * norm_scale).astype(jnp.bfloat16)
    cell_cosine, cell_sine = rope_tables(jnp.arange(cell_number), HEAD_WIDTH // 2)
    head_cosine, head_sine = rope_tables(header_positions, HEAD_WIDTH // 2)
    projected_rows = jnp.dot(normed, query_full, preferred_element_type=jnp.float32).reshape(cell_number, HQ, HEAD_WIDTH)
    query_matrix = apply_rotary(projected_rows, cell_cosine, cell_sine).astype(jnp.bfloat16).reshape(cell_number, KEY_HEADS, QUERY_PER_KV, HEAD_WIDTH)
    keys_rotated = apply_rotary(unrotated_keys.astype(jnp.float32).reshape(-1, KEY_HEADS, HEAD_WIDTH), head_cosine, head_sine).astype(jnp.bfloat16)
    header_value_rows = plain_values.reshape(-1, KEY_HEADS, HEAD_WIDTH)
    total_heads = keys_rotated.shape[0]
    allowed = (segments[:, None] == (jnp.arange(total_heads) // HPS)[None, :]).astype(jnp.float32)
    scores = jnp.einsum('ngjd,kgd->gjnk', query_matrix.astype(jnp.float32), keys_rotated.astype(jnp.float32)) * score_scale
    weights_exp = jnp.exp(scores) * allowed
    probabilities = (weights_exp / lax.optimization_barrier(jnp.sum(weights_exp, axis=-1, keepdims=True))).astype(jnp.bfloat16)
    head_gradients = jnp.dot(grad_output, output_full.T, preferred_element_type=jnp.float32).astype(jnp.bfloat16)
    head_gradients = head_gradients.reshape(cell_number, KEY_HEADS, QUERY_PER_KV, HEAD_WIDTH)
    grad_probs = jnp.einsum('ngjd,kgd->gjnk', head_gradients.astype(jnp.float32), header_value_rows.astype(jnp.float32))
    broad_probs = probabilities.astype(jnp.float32)
    row_total = lax.optimization_barrier(jnp.sum(broad_probs * grad_probs, axis=-1, keepdims=True))
    grad_scores = (broad_probs * (grad_probs - row_total) * score_scale).astype(jnp.bfloat16)
    grad_rot = jnp.einsum('gjnk,kgd->ngjd', grad_scores.astype(jnp.float32), keys_rotated.astype(jnp.float32))
    grad_rot = grad_rot.reshape(cell_number, HQ, HEAD_WIDTH)
    grad_query = apply_rotary(grad_rot, cell_cosine, -cell_sine).astype(jnp.bfloat16).reshape(cell_number, HQ * HEAD_WIDTH)
    grad_normed = jnp.dot(grad_query, query_full.T, preferred_element_type=jnp.float32)
    scaled = grad_normed * norm_scale
    grad_input = grad_output.astype(jnp.float32) + inv_rms * scaled - widened * inv_rms ** 3 * lax.optimization_barrier(jnp.mean(widened * scaled, axis=-1, keepdims=True))
    key_rotated = jnp.einsum('uohb,huox->bux', grad_scores.astype(jnp.float32), query_matrix.astype(jnp.float32))
    header_key_gradient = apply_rotary(key_rotated, head_cosine, -head_sine).reshape(total_heads, KEY_HEADS * HEAD_WIDTH)
    header_value_gradient = jnp.einsum('uohb,huox->bux', broad_probs, head_gradients.astype(jnp.float32)).reshape(total_heads, KEY_HEADS * HEAD_WIDTH)
    return (grad_input.astype(jnp.bfloat16), header_key_gradient, header_value_gradient)

def reference(section_input, out_grad, norm_gain, query_weight, output_weight, header_keys, header_values, header_pos, segment_ids):
    input_rows = [[None] * MB for section_index in range(N_SECTION)]
    key_rows = [[None] * MB for section_index in range(N_SECTION)]
    value_rows = [[None] * MB for section_index in range(N_SECTION)]
    for micro_index in range(MB):
        grad_output = out_grad[micro_index]
        for section_index in reversed(range(N_SECTION)):
            grad_input, header_key_gradient, header_value_gradient = layer_backward(section_input[section_index, micro_index], norm_gain[section_index], query_weight[section_index], output_weight[section_index], header_keys[section_index, micro_index], header_values[section_index, micro_index], header_pos[micro_index], segment_ids[micro_index], grad_output)
            input_rows[section_index][micro_index] = grad_input
            key_rows[section_index][micro_index] = header_key_gradient
            value_rows[section_index][micro_index] = header_value_gradient
            grad_output = grad_input
    grad_all = jnp.stack([jnp.stack(section_list) for section_list in input_rows])
    key_all = jnp.stack([jnp.stack(section_list) for section_list in key_rows])
    value_all = jnp.stack([jnp.stack(section_list) for section_list in value_rows])
    return (grad_all, key_all, value_all)
```

```python
import functools
import math

import jax
import jax.numpy as jnp
from jax import lax
from jax.experimental import pallas as pl
from jax.experimental.pallas import tpu as pltpu
from jax.sharding import PartitionSpec as P

KEY_HEADS = 4
HEAD_WIDTH = 64
HPS = 8
GROUP = 4
LANES = GROUP * HEAD_WIDTH

EPSILON = 1e-05
ROPE_BASE = 500000.0
MESH = pl.DeviceIdType.MESH
NT = (((1,), (1,)), ((), ()))
TN = (((0,), (0,)), ((), ()))
NN = (((1,), (0,)), ((), ()))
F32 = jnp.float32
BF16 = jnp.bfloat16


def mm(a, b, dims):
    return lax.dot_general(a, b, dims, preferred_element_type=F32)


def rope_wide(positions):
    half = HEAD_WIDTH // 2
    freq_index = jnp.arange(half, dtype=F32)
    inverse = jnp.exp(freq_index * (-2.0 * math.log(ROPE_BASE) / (2 * half)))
    angles = positions.astype(F32)[..., None] * inverse
    cosine, sine = jnp.cos(angles), jnp.sin(angles)
    wide_cos = jnp.concatenate([cosine, cosine] * GROUP, axis=-1)
    wide_sin = jnp.concatenate([-sine, sine] * GROUP, axis=-1)
    return wide_cos, wide_sin


def half_swap(v):
    width = v.shape[1]
    half = HEAD_WIDTH // 2
    lane = lax.broadcasted_iota(jnp.int32, v.shape, 1)
    from_right = pltpu.roll(v, width - half, 1)
    from_left = pltpu.roll(v, half, 1)
    return jnp.where(lane % HEAD_WIDTH < half, from_right, from_left)


def rotate(v, cosine, signed_sine):
    return v * cosine + half_swap(v) * signed_sine


def fold_heads(v):
    v = v + pltpu.roll(v, 2 * HEAD_WIDTH, 1)
    return v + pltpu.roll(v, HEAD_WIDTH, 1)


def block_sum(v, ones_block):
    high = v.astype(BF16)
    low = (v - high.astype(F32)).astype(BF16)
    return mm(high, ones_block, NN) + mm(low, ones_block, NN)


def kernel(
    n, sections, *refs
):
    (
        x_ref, og_ref, gain_ref, wq_ref, wo_ref, hdr_ref, cos_ref, sin_ref, hcos_ref, hsin_ref, seg_ref,
        gi_ref, ko_ref, vo_ref,
        wq_s, wo_s, hdr_s, hd_s, kb_s, vb_s, normed_s, inv_s, q_s, p_s, gin_s, gq_s, gn_s, acc_s, part_s, rs_s,
        ssem, rsem, hs_sem, hr_sem, gs_sem, gr_sem, rss_sem, rsr_sem,
    ) = refs
    me = lax.axis_index("seq")
    sec = lax.axis_index("section")
    mbs, rows, width = x_ref.shape
    heads = hcos_ref.shape[1]
    own_heads = heads // n
    span = GROUP * heads
    line = n // 4
    a, b, c = me // 4, (me // 2) % 2, me % 2

    barrier = pltpu.get_barrier_semaphore()

    @pl.loop(1, n)
    def _(d):
        pl.semaphore_signal(barrier, inc=1, device_id={"seq": (me + d) % n}, device_id_type=MESH)

    @pl.when(sec > 0)
    def _():
        pl.semaphore_signal(barrier, inc=1, device_id={"section": sec - 1}, device_id_type=MESH)

    @pl.when(sec < sections - 1)
    def _():
        pl.semaphore_signal(barrier, inc=1, device_id={"section": sec + 1}, device_id_type=MESH)

    rq, ro = wq_ref.shape[0], wo_ref.shape[0]
    wq_s[pl.ds(pl.multiple_of(me * rq, rq), rq), :] = wq_ref[...]
    wo_s[pl.ds(pl.multiple_of(me * ro, ro), ro), :] = wo_ref[...]
    hdr_s[me] = hdr_ref[...]
    neighbours = (sec > 0).astype(jnp.int32) + (sec < sections - 1).astype(jnp.int32)
    pl.semaphore_wait(barrier, n - 1 + neighbours)

    def spot(aa, bb, cc):
        return aa * 4 + bb * 2 + cc

    def block(w, owner):
        scr, r = ((wq_s, rq), (wo_s, ro))[w]
        return scr.at[pl.ds(pl.multiple_of(owner * r, r), r), :]

    def copy(w, owner, send, recv, target):
        return pltpu.make_async_remote_copy(
            src_ref=block(w, owner),
            dst_ref=block(w, owner),
            send_sem=ssem.at[w, send[0], send[1]],
            recv_sem=rsem.at[w, recv[0], recv[1]],
            device_id={"seq": target},
            device_id_type=MESH,
        )

    def owner_line(slot):
        return a - slot if slot < line else a + (slot - line + 1)

    def valid(slot):
        if slot == 0:
            return a >= 0
        return (a >= slot) if slot < line else (a + (slot - line + 1) < line)

    def up(w, slot):
        return copy(w, spot(owner_line(slot), b, c), (0, slot), (0, slot + 1), spot(a + 1, b, c))

    def down(w, slot):
        later = line if slot == 0 else slot + 1
        return copy(w, spot(owner_line(slot), b, c), (1, slot), (0, later), spot(a - 1, b, c))

    def across(w, slot):
        return copy(w, spot(owner_line(slot), b, c), (2, slot), (1, slot), spot(a, 1 - b, c))

    def core_a(w, slot):
        return copy(w, spot(owner_line(slot), b, c), (3, slot), (2, slot), spot(a, b, 1 - c))

    def core_b(w, slot):
        return copy(w, spot(owner_line(slot), 1 - b, c), (4, slot), (3, slot), spot(a, b, 1 - c))

    def arrived(w, owner, kind, slot):
        copy(w, owner, (0, 0), (kind, slot), spot(a, b, 1 - c)).wait_recv()

    def goes_up(slot):
        return slot < line - 1

    def goes_down(slot):
        return slot == 0 or (line <= slot and slot < 2 * line - 2)

    def send_on(w, slot):
        if goes_up(slot):
            pl.when(valid(slot) & (a + 1 < line))(lambda: up(w, slot).start())
        if goes_down(slot):
            pl.when(valid(slot) & (a > 0))(lambda: down(w, slot).start())

        @pl.when(valid(slot))
        def _():
            across(w, slot).start()
            core_a(w, slot).start()

    def take_line(w, slot):
        pl.when(valid(slot))(lambda: arrived(w, spot(owner_line(slot), b, c), 0, slot))
        send_on(w, slot)

    def take_across(w, slot):
        @pl.when(valid(slot))
        def _():
            arrived(w, spot(owner_line(slot), 1 - b, c), 1, slot)
            core_b(w, slot).start()

    def take_core(w, slot):
        @pl.when(valid(slot))
        def _():
            arrived(w, spot(owner_line(slot), b, 1 - c), 2, slot)
            arrived(w, spot(owner_line(slot), 1 - b, 1 - c), 3, slot)

    def finish(w, slot):
        if goes_up(slot):
            pl.when(valid(slot) & (a + 1 < line))(lambda: up(w, slot).wait_send())
        if goes_down(slot):
            pl.when(valid(slot) & (a > 0))(lambda: down(w, slot).wait_send())

        @pl.when(valid(slot))
        def _():
            across(w, slot).wait_send()
            core_a(w, slot).wait_send()
            core_b(w, slot).wait_send()

    def slots_of(k):
        return [0] if k == 0 else [k, line - 1 + k]

    def header_copy(d):
        return pltpu.make_async_remote_copy(
            src_ref=hdr_s.at[me],
            dst_ref=hdr_s.at[me],
            send_sem=hs_sem.at[d],
            recv_sem=hr_sem.at[d],
            device_id={"seq": (me + d) % n},
            device_id_type=MESH,
        )

    def header_arrival(d):
        source = (me + n - d) % n
        return pltpu.make_async_remote_copy(
            src_ref=hdr_s.at[source],
            dst_ref=hdr_s.at[source],
            send_sem=hs_sem.at[d],
            recv_sem=hr_sem.at[d],
            device_id={"seq": (me + d) % n},
            device_id_type=MESH,
        )

    pl.loop(1, n)(lambda d: header_copy(d).start())
    for w in (0, 1):
        send_on(w, 0)

    for m in range(mbs):
        wide = x_ref[m].astype(F32)
        inv = lax.rsqrt(jnp.mean(wide * wide, axis=-1, keepdims=True) + EPSILON)
        inv_s[m] = jnp.broadcast_to(inv, (rows, 128))
        normed_s[m * rows:(m + 1) * rows, :] = (wide * inv * gain_ref[...]).astype(BF16)

    @pl.when(sec == sections - 1)
    def _():
        gin_s[...] = og_ref[...]

    pl.loop(1, n)(lambda d: header_arrival(d).wait_recv())
    for i in range(n):
        for j in range(2 * mbs):
            hd_s[j, i * own_heads:(i + 1) * own_heads, :] = hdr_s[i, j * own_heads:(j + 1) * own_heads, :]
    lane = lax.broadcasted_iota(jnp.int32, (heads, LANES), 1) // HEAD_WIDTH

    def spread(v, g):
        return fold_heads(jnp.where(lane == g, v, 0.0))

    for m in range(mbs):
        keys = rotate(hd_s[m], hcos_ref[m], hsin_ref[m]).astype(BF16).astype(F32)
        values = hd_s[mbs + m]
        for g in range(KEY_HEADS):
            wide_k, wide_v = spread(keys, g), spread(values, g)
            for j in range(GROUP):
                kb_s[m, g, j * heads:(j + 1) * heads, :] = jnp.where(lane == j, wide_k, 0.0).astype(BF16)
                vb_s[m, g, j * heads:(j + 1) * heads, :] = jnp.where(lane == j, wide_v, 0.0).astype(BF16)

    for k in range(1, line):
        for w in (0, 1):
            for slot in slots_of(k):
                take_line(w, slot)
            for slot in slots_of(k - 1):
                take_across(w, slot)
    for w in (0, 1):
        for slot in slots_of(line - 1):
            take_across(w, slot)
        for k in range(line):
            for slot in slots_of(k):
                take_core(w, slot)

    ones_block = (
        lax.broadcasted_iota(jnp.int32, (span, span), 0) // heads
        == lax.broadcasted_iota(jnp.int32, (span, span), 1) // heads
    ).astype(F32).astype(BF16)
    column = lax.broadcasted_iota(jnp.int32, (rows, span), 1)
    column_segment = (column % heads) // HPS
    cosine, sine = cos_ref[...], sin_ref[...]
    scale = HEAD_WIDTH ** (-0.5)

    @pl.loop(0, KEY_HEADS)
    def _(g):
        cols = pl.ds(pl.multiple_of(g * LANES, LANES), LANES)
        wide_cols = pl.ds(pl.multiple_of(g * span, 128), span)
        projected = mm(normed_s[...], wq_s[:, cols], NN)
        for m in range(mbs):
            query = rotate(projected[m * rows:(m + 1) * rows], cosine, sine).astype(BF16)
            q_s[m, :, cols] = query
            score = mm(query, kb_s[m, g], NT) * scale
            segment = jnp.concatenate([seg_ref[m]] * (span // 128), axis=1)
            weight = jnp.where(segment == column_segment, jnp.exp(score), 0.0)
            p_s[m, :, wide_cols] = (weight / block_sum(weight, ones_block)).astype(BF16)

    diag = (
        lax.broadcasted_iota(jnp.int32, (span, LANES), 0) // heads
        == lax.broadcasted_iota(jnp.int32, (span, LANES), 1) // HEAD_WIDTH
    )

    def folded(product):
        kept = jnp.where(diag, product, 0.0)
        total = kept[0:heads]
        for j in range(1, GROUP):
            total = total + kept[j * heads:(j + 1) * heads]
        return fold_heads(total)

    def pass_grad(m):
        return pltpu.make_async_remote_copy(
            src_ref=gi_ref.at[m],
            dst_ref=gin_s.at[m],
            send_sem=gs_sem.at[m],
            recv_sem=gr_sem.at[m],
            device_id={"section": jnp.maximum(sec - 1, 0)},
            device_id_type=MESH,
        )

    def part_copy(m, d):
        return pltpu.make_async_remote_copy(
            src_ref=part_s.at[m, (me + d) % n],
            dst_ref=rs_s.at[m, d],
            send_sem=rss_sem.at[m, d],
            recv_sem=rsr_sem.at[m, d],
            device_id={"seq": (me + d) % n},
            device_id_type=MESH,
        )

    tile = 256
    for m in range(mbs):
        pl.when(sec < sections - 1)(lambda: pass_grad(m).wait_recv())
        acc_s[...] = jnp.zeros_like(acc_s)

        @pl.loop(0, KEY_HEADS)
        def _(g):
            cols = pl.ds(pl.multiple_of(g * LANES, LANES), LANES)
            wide_cols = pl.ds(pl.multiple_of(g * span, 128), span)
            head_grad = mm(gin_s[m], wo_s[cols, :], NT).astype(BF16)
            probs = p_s[m, :, wide_cols]
            broad = probs.astype(F32)
            grad_probs = mm(head_grad, vb_s[m, g], NT)
            row_total = block_sum(broad * grad_probs, ones_block)
            grad_scores = (broad * (grad_probs - row_total) * scale).astype(BF16)
            grad_rot = mm(grad_scores, kb_s[m, g], NN)
            gq_s[:, cols] = rotate(grad_rot, cosine, -sine).astype(BF16)
            key_part = folded(mm(grad_scores, q_s[m, :, cols], TN))
            value_part = folded(mm(probs, head_grad, TN))
            here = lane == g
            acc_s[0] = jnp.where(here, key_part, acc_s[0])
            acc_s[1] = jnp.where(here, value_part, acc_s[1])

        @pl.loop(0, width // tile)
        def _(t):
            cols = pl.ds(pl.multiple_of(t * tile, tile), tile)
            gn_s[:, cols] = mm(gq_s[...], wq_s[cols, :], NT) * gain_ref[:, cols]

        wide = x_ref[m].astype(F32)
        scaled = gn_s[...]
        inv = inv_s[m][:, 0:1]
        mean = jnp.mean(wide * scaled, axis=-1, keepdims=True)
        gi_ref[m] = (
            gin_s[m].astype(F32) + inv * scaled - wide * (inv * inv * inv * mean)
        ).astype(BF16)
        pl.when(sec > 0)(lambda: pass_grad(m).start())

        key_total = rotate(acc_s[0], hcos_ref[m], -hsin_ref[m])
        value_total = acc_s[1]
        for i in range(n):
            part_s[m, i, 0:own_heads, :] = key_total[i * own_heads:(i + 1) * own_heads]
            part_s[m, i, own_heads:2 * own_heads, :] = value_total[i * own_heads:(i + 1) * own_heads]
        pl.loop(1, n)(lambda d: part_copy(m, d).start())

    for m in range(mbs):
        pl.loop(1, n)(lambda d: part_copy(m, d).wait_recv())
        rs_s[m, 0] = part_s[m, me]
        total = jnp.sum(rs_s[m], axis=0)
        ko_ref[m] = total[0:own_heads]
        vo_ref[m] = total[own_heads:2 * own_heads]
    for m in range(mbs):
        pl.loop(1, n)(lambda d: part_copy(m, d).wait_send())
        pl.when(sec > 0)(lambda: pass_grad(m).wait_send())
    pl.loop(1, n)(lambda d: header_copy(d).wait_send())
    for w in (0, 1):
        for k in range(line):
            for slot in slots_of(k):
                finish(w, slot)


def per_device(
    section_input,
    out_grad,
    norm_gain,
    query_weight,
    output_weight,
    header_keys,
    header_values,
    header_pos,
    segment_ids,
):
    sections = lax.axis_size("section")
    n = lax.axis_size("seq")
    me = lax.axis_index("seq")
    mbs, rows, width = section_input.shape[1:]
    own_heads, kv_width = header_keys.shape[2:]
    heads = own_heads * n
    span = GROUP * heads
    qw = query_weight.shape[2]
    slots = 2 * (n // 4) - 1
    headers = jnp.concatenate(
        [header_keys[0].reshape(-1, kv_width), header_values[0].reshape(-1, kv_width)], axis=0
    ).astype(F32)
    cosine, sine = rope_wide(me * rows + jnp.arange(rows, dtype=jnp.int32))
    hcos, hsin = rope_wide(header_pos)
    segments = jnp.broadcast_to(segment_ids[:, :, None], (mbs, rows, 128))
    vmem = pl.BlockSpec(memory_space=pltpu.VMEM)
    dma = pltpu.SemaphoreType.DMA
    grads, keys, values = pl.pallas_call(
        functools.partial(kernel, n, sections),
        out_shape=(
            jax.ShapeDtypeStruct((mbs, rows, width), BF16),
            jax.ShapeDtypeStruct((mbs, own_heads, kv_width), F32),
            jax.ShapeDtypeStruct((mbs, own_heads, kv_width), F32),
        ),
        in_specs=[vmem] * 11,
        out_specs=[vmem] * 3,
        scratch_shapes=[
            pltpu.VMEM((width, qw), BF16),
            pltpu.VMEM((qw, width), BF16),
            pltpu.VMEM((n, 2 * mbs * own_heads, kv_width), F32),
            pltpu.VMEM((2 * mbs, heads, kv_width), F32),
            pltpu.VMEM((mbs, KEY_HEADS, span, LANES), BF16),
            pltpu.VMEM((mbs, KEY_HEADS, span, LANES), BF16),
            pltpu.VMEM((mbs * rows, width), BF16),
            pltpu.VMEM((mbs, rows, 128), F32),
            pltpu.VMEM((mbs, rows, qw), BF16),
            pltpu.VMEM((mbs, rows, KEY_HEADS * span), BF16),
            pltpu.VMEM((mbs, rows, width), BF16),
            pltpu.VMEM((rows, qw), BF16),
            pltpu.VMEM((rows, width), F32),
            pltpu.VMEM((2, heads, kv_width), F32),
            pltpu.VMEM((mbs, n, 2 * own_heads, kv_width), F32),
            pltpu.VMEM((mbs, n, 2 * own_heads, kv_width), F32),
            dma((2, 5, slots)),
            dma((2, 4, slots)),
            dma((n,)),
            dma((n,)),
            dma((mbs,)),
            dma((mbs,)),
            dma((mbs, n)),
            dma((mbs, n)),
        ],
        compiler_params=pltpu.CompilerParams(
            collective_id=0, has_side_effects=True, vmem_limit_bytes=56 << 20
        ),
        name="relay_backward",
    )(
        section_input[0], out_grad, norm_gain, query_weight[0], output_weight[0],
        headers, cosine, sine, hcos, hsin, segments,
    )
    return (grads[None], keys[None], values[None])


def solution(mesh):
    in_specs = (
        P("section", None, "seq", None),
        P(None, "seq", None),
        P("section", None),
        P("section", "seq", None),
        P("section", "seq", None),
        P("section", None, "seq", None),
        P("section", None, "seq", None),
        P(),
        P(None, "seq"),
    )
    out_specs = (
        P("section", None, "seq", None),
        P("section", None, "seq", None),
        P("section", None, "seq", None),
    )
    return jax.shard_map(
        per_device, mesh=mesh, in_specs=in_specs, out_specs=out_specs, check_vma=False
    )
```

```python
import functools
import math

import jax
import jax.numpy as jnp
from jax import lax
from jax.experimental import pallas as pl
from jax.experimental.pallas import tpu as pltpu
from jax.sharding import PartitionSpec as P

KEY_HEADS = 4
HEAD_WIDTH = 64
HPS = 8
GROUP = 4
LANES = GROUP * HEAD_WIDTH

EPSILON = 1e-05
ROPE_BASE = 500000.0
MESH = pl.DeviceIdType.MESH
NT = (((1,), (1,)), ((), ()))
TN = (((0,), (0,)), ((), ()))
NN = (((1,), (0,)), ((), ()))
F32 = jnp.float32
BF16 = jnp.bfloat16


def mm(a, b, dims):
    return lax.dot_general(a, b, dims, preferred_element_type=F32)


def as_column(row):
    k = row.shape[1]
    same = lax.broadcasted_iota(jnp.int32, (k, k), 0) == lax.broadcasted_iota(jnp.int32, (k, k), 1)
    return jnp.sum(jnp.where(same, row, 0.0), axis=1, keepdims=True)


def rope_wide(positions):
    half = HEAD_WIDTH // 2
    lane = lax.broadcasted_iota(jnp.int32, (positions.shape[0], 128), 1)
    inverse = jnp.exp((lane % half).astype(F32) * (-2.0 * math.log(ROPE_BASE) / (2 * half)))
    angles = positions * inverse
    cosine, sine = jnp.cos(angles), jnp.sin(angles)
    sine = jnp.where(lane % HEAD_WIDTH < half, -sine, sine)
    return jnp.concatenate([cosine] * (LANES // 128), axis=1), jnp.concatenate([sine] * (LANES // 128), axis=1)


def half_swap(v):
    width = v.shape[1]
    half = HEAD_WIDTH // 2
    lane = lax.broadcasted_iota(jnp.int32, v.shape, 1)
    from_right = pltpu.roll(v, width - half, 1)
    from_left = pltpu.roll(v, half, 1)
    return jnp.where(lane % HEAD_WIDTH < half, from_right, from_left)


def rotate(v, cosine, signed_sine):
    return v * cosine + half_swap(v) * signed_sine


def fold_heads(v):
    v = v + pltpu.roll(v, 2 * HEAD_WIDTH, 1)
    return v + pltpu.roll(v, HEAD_WIDTH, 1)


def block_sum(v, ones_block):
    high = v.astype(BF16)
    low = (v - high.astype(F32)).astype(BF16)
    return mm(high, ones_block, NN) + mm(low, ones_block, NN)


def kernel(
    n, sections, *refs
):
    (
        x_ref, og_ref, gain_ref, wq_ref, wo_ref, hk_ref, hv_ref, pos_ref, seg_ref,
        gi_ref, ko_ref, vo_ref,
        wq_s, wo_s, hdr_s, hd_s, kb_s, vb_s, normed_s, inv_s, cos_s, sin_s, hcos_s, hsin_s, q_s, p_s, gin_s, gq_s, gn_s, acc_s, part_s, rs_s,
        ssem, rsem, hs_sem, hr_sem, gs_sem, gr_sem, rss_sem, rsr_sem,
    ) = refs
    me = lax.axis_index("seq")
    sec = lax.axis_index("section")
    mbs, rows, width = x_ref.shape
    heads = pos_ref.shape[1]
    own_heads = heads // n
    span = GROUP * heads
    line = n // 4
    a, b, c = me // 4, (me // 2) % 2, me % 2

    barrier = pltpu.get_barrier_semaphore()

    @pl.loop(1, n)
    def _(d):
        pl.semaphore_signal(barrier, inc=1, device_id={"seq": (me + d) % n}, device_id_type=MESH)

    @pl.when(sec > 0)
    def _():
        pl.semaphore_signal(barrier, inc=1, device_id={"section": sec - 1}, device_id_type=MESH)

    @pl.when(sec < sections - 1)
    def _():
        pl.semaphore_signal(barrier, inc=1, device_id={"section": sec + 1}, device_id_type=MESH)

    rq, ro = wq_ref.shape[0], wo_ref.shape[0]
    wq_s[pl.ds(pl.multiple_of(me * rq, rq), rq), :] = wq_ref[...]
    wo_s[pl.ds(pl.multiple_of(me * ro, ro), ro), :] = wo_ref[...]
    own_headers = [hk_ref[m].astype(F32) for m in range(mbs)] + [hv_ref[m].astype(F32) for m in range(mbs)]
    hdr_s[me] = jnp.concatenate(own_headers, axis=0)
    neighbours = (sec > 0).astype(jnp.int32) + (sec < sections - 1).astype(jnp.int32)
    pl.semaphore_wait(barrier, n - 1 + neighbours)

    def spot(aa, bb, cc):
        return aa * 4 + bb * 2 + cc

    def block(w, owner):
        scr, r = ((wq_s, rq), (wo_s, ro))[w]
        return scr.at[pl.ds(pl.multiple_of(owner * r, r), r), :]

    def copy(w, owner, send, recv, target):
        return pltpu.make_async_remote_copy(
            src_ref=block(w, owner),
            dst_ref=block(w, owner),
            send_sem=ssem.at[w, send[0], send[1]],
            recv_sem=rsem.at[w, recv[0], recv[1]],
            device_id={"seq": target},
            device_id_type=MESH,
        )

    def owner_line(slot):
        return a - slot if slot < line else a + (slot - line + 1)

    def valid(slot):
        if slot == 0:
            return a >= 0
        return (a >= slot) if slot < line else (a + (slot - line + 1) < line)

    def up(w, slot):
        return copy(w, spot(owner_line(slot), b, c), (0, slot), (0, slot + 1), spot(a + 1, b, c))

    def down(w, slot):
        later = line if slot == 0 else slot + 1
        return copy(w, spot(owner_line(slot), b, c), (1, slot), (0, later), spot(a - 1, b, c))

    def across(w, slot):
        return copy(w, spot(owner_line(slot), b, c), (2, slot), (1, slot), spot(a, 1 - b, c))

    def core_a(w, slot):
        return copy(w, spot(owner_line(slot), b, c), (3, slot), (2, slot), spot(a, b, 1 - c))

    def core_b(w, slot):
        return copy(w, spot(owner_line(slot), 1 - b, c), (4, slot), (3, slot), spot(a, b, 1 - c))

    def arrived(w, owner, kind, slot):
        copy(w, owner, (0, 0), (kind, slot), spot(a, b, 1 - c)).wait_recv()

    def goes_up(slot):
        return slot < line - 1

    def goes_down(slot):
        return slot == 0 or (line <= slot and slot < 2 * line - 2)

    def send_on(w, slot):
        if goes_up(slot):
            pl.when(valid(slot) & (a + 1 < line))(lambda: up(w, slot).start())
        if goes_down(slot):
            pl.when(valid(slot) & (a > 0))(lambda: down(w, slot).start())

        @pl.when(valid(slot))
        def _():
            across(w, slot).start()
            core_a(w, slot).start()

    def take_line(w, slot):
        pl.when(valid(slot))(lambda: arrived(w, spot(owner_line(slot), b, c), 0, slot))
        send_on(w, slot)

    def take_across(w, slot):
        @pl.when(valid(slot))
        def _():
            arrived(w, spot(owner_line(slot), 1 - b, c), 1, slot)
            core_b(w, slot).start()

    def take_core(w, slot):
        @pl.when(valid(slot))
        def _():
            arrived(w, spot(owner_line(slot), b, 1 - c), 2, slot)
            arrived(w, spot(owner_line(slot), 1 - b, 1 - c), 3, slot)

    def finish(w, slot):
        if goes_up(slot):
            pl.when(valid(slot) & (a + 1 < line))(lambda: up(w, slot).wait_send())
        if goes_down(slot):
            pl.when(valid(slot) & (a > 0))(lambda: down(w, slot).wait_send())

        @pl.when(valid(slot))
        def _():
            across(w, slot).wait_send()
            core_a(w, slot).wait_send()
            core_b(w, slot).wait_send()

    def slots_of(k):
        return [0] if k == 0 else [k, line - 1 + k]

    def header_copy(d):
        return pltpu.make_async_remote_copy(
            src_ref=hdr_s.at[me],
            dst_ref=hdr_s.at[me],
            send_sem=hs_sem.at[d],
            recv_sem=hr_sem.at[d],
            device_id={"seq": (me + d) % n},
            device_id_type=MESH,
        )

    def header_arrival(d):
        source = (me + n - d) % n
        return pltpu.make_async_remote_copy(
            src_ref=hdr_s.at[source],
            dst_ref=hdr_s.at[source],
            send_sem=hs_sem.at[d],
            recv_sem=hr_sem.at[d],
            device_id={"seq": (me + d) % n},
            device_id_type=MESH,
        )

    pl.loop(1, n)(lambda d: header_copy(d).start())
    for w in (0, 1):
        send_on(w, 0)

    for m in range(mbs):
        wide = x_ref[m].astype(F32)
        inv = lax.rsqrt(jnp.mean(wide * wide, axis=-1, keepdims=True) + EPSILON)
        inv_s[m] = jnp.broadcast_to(inv, (rows, 128))
        normed_s[m * rows:(m + 1) * rows, :] = (wide * inv * gain_ref[...]).astype(BF16)

    @pl.when(sec == sections - 1)
    def _():
        gin_s[...] = og_ref[...]

    cos_s[...], sin_s[...] = rope_wide(
        (me * rows + lax.broadcasted_iota(jnp.int32, (rows, 1), 0)).astype(F32)
    )
    for m in range(mbs):
        hcos_s[m], hsin_s[m] = rope_wide(as_column(pos_ref[m:m + 1, :].astype(F32)))

    pl.loop(1, n)(lambda d: header_arrival(d).wait_recv())
    for i in range(n):
        for j in range(2 * mbs):
            hd_s[j, i * own_heads:(i + 1) * own_heads, :] = hdr_s[i, j * own_heads:(j + 1) * own_heads, :]
    lane = lax.broadcasted_iota(jnp.int32, (heads, LANES), 1) // HEAD_WIDTH

    def spread(v, g):
        return fold_heads(jnp.where(lane == g, v, 0.0))

    for m in range(mbs):
        keys = rotate(hd_s[m], hcos_s[m], hsin_s[m]).astype(BF16).astype(F32)
        values = hd_s[mbs + m]
        for g in range(KEY_HEADS):
            wide_k, wide_v = spread(keys, g), spread(values, g)
            for j in range(GROUP):
                kb_s[m, g, j * heads:(j + 1) * heads, :] = jnp.where(lane == j, wide_k, 0.0).astype(BF16)
                vb_s[m, g, j * heads:(j + 1) * heads, :] = jnp.where(lane == j, wide_v, 0.0).astype(BF16)

    ones_block = (
        lax.broadcasted_iota(jnp.int32, (span, span), 0) // heads
        == lax.broadcasted_iota(jnp.int32, (span, span), 1) // heads
    ).astype(F32).astype(BF16)
    column = lax.broadcasted_iota(jnp.int32, (rows, span), 1)
    column_segment = (column % heads) // HPS
    cosine, sine = cos_s[...], sin_s[...]
    segment_columns = [as_column(seg_ref[m:m + 1, :].astype(F32)).astype(jnp.int32) for m in range(mbs)]
    scale = HEAD_WIDTH ** (-0.5)

    def forward(g):
        cols = slice(g * LANES, (g + 1) * LANES)
        projected = mm(normed_s[...], wq_s[:, cols], NN)
        for m in range(mbs):
            query = rotate(projected[m * rows:(m + 1) * rows], cosine, sine).astype(BF16)
            q_s[m, :, cols] = query
            score = mm(query, kb_s[m, g], NT) * scale
            weight = jnp.where(segment_columns[m] == column_segment, jnp.exp(score), 0.0)
            p_s[m, :, g * span:(g + 1) * span] = (weight / block_sum(weight, ones_block)).astype(BF16)

    def relay(w, k):
        for slot in slots_of(k):
            take_line(w, slot)
        for slot in slots_of(k - 1):
            take_across(w, slot)

    def last_across(w):
        for slot in slots_of(line - 1):
            take_across(w, slot)

    def all_core(w):
        for k in range(line):
            for slot in slots_of(k):
                take_core(w, slot)

    for k in range(1, line):
        relay(0, k)
        if k > 1:
            relay(1, k - 1)
    last_across(0)
    all_core(0)
    forward(0)
    relay(1, line - 1)
    forward(1)
    last_across(1)
    for g in range(2, KEY_HEADS):
        forward(g)
    all_core(1)

    diag = (
        lax.broadcasted_iota(jnp.int32, (span, LANES), 0) // heads
        == lax.broadcasted_iota(jnp.int32, (span, LANES), 1) // HEAD_WIDTH
    )

    def folded(product):
        kept = jnp.where(diag, product, 0.0)
        total = kept[0:heads]
        for j in range(1, GROUP):
            total = total + kept[j * heads:(j + 1) * heads]
        return fold_heads(total)

    def pass_grad(m):
        return pltpu.make_async_remote_copy(
            src_ref=gi_ref.at[m],
            dst_ref=gin_s.at[m],
            send_sem=gs_sem.at[m],
            recv_sem=gr_sem.at[m],
            device_id={"section": jnp.maximum(sec - 1, 0)},
            device_id_type=MESH,
        )

    def part_copy(m, d):
        return pltpu.make_async_remote_copy(
            src_ref=part_s.at[m, (me + d) % n],
            dst_ref=rs_s.at[m, d],
            send_sem=rss_sem.at[m, d],
            recv_sem=rsr_sem.at[m, d],
            device_id={"seq": (me + d) % n},
            device_id_type=MESH,
        )

    def scatter(m):
        key_total = rotate(acc_s[0], hcos_s[m], -hsin_s[m])
        value_total = acc_s[1]
        for i in range(n):
            part_s[m, i, 0:own_heads, :] = key_total[i * own_heads:(i + 1) * own_heads]
            part_s[m, i, own_heads:2 * own_heads, :] = value_total[i * own_heads:(i + 1) * own_heads]
        pl.loop(1, n)(lambda d: part_copy(m, d).start())

    tile = 256
    for m in range(mbs):
        pl.when(sec < sections - 1)(lambda: pass_grad(m).wait_recv())
        acc_s[...] = jnp.zeros_like(acc_s)

        for g in range(KEY_HEADS):
            cols = slice(g * LANES, (g + 1) * LANES)
            wide_cols = slice(g * span, (g + 1) * span)
            head_grad = mm(gin_s[m], wo_s[cols, :], NT).astype(BF16)
            probs = p_s[m, :, wide_cols]
            broad = probs.astype(F32)
            grad_probs = mm(head_grad, vb_s[m, g], NT)
            row_total = block_sum(broad * grad_probs, ones_block)
            grad_scores = (broad * (grad_probs - row_total) * scale).astype(BF16)
            grad_rot = mm(grad_scores, kb_s[m, g], NN)
            gq_s[:, cols] = rotate(grad_rot, cosine, -sine).astype(BF16)
            key_part = folded(mm(grad_scores, q_s[m, :, cols], TN))
            value_part = folded(mm(probs, head_grad, TN))
            here = lane == g
            acc_s[0] = jnp.where(here, key_part, acc_s[0])
            acc_s[1] = jnp.where(here, value_part, acc_s[1])

        if m == mbs - 1:
            scatter(m)

        for t in range(width // tile):
            cols = slice(t * tile, (t + 1) * tile)
            gn_s[:, cols] = mm(gq_s[...], wq_s[cols, :], NT) * gain_ref[:, cols]

        wide = x_ref[m].astype(F32)
        scaled = gn_s[...]
        inv = inv_s[m][:, 0:1]
        mean = jnp.mean(wide * scaled, axis=-1, keepdims=True)
        gi_ref[m] = (
            gin_s[m].astype(F32) + inv * scaled - wide * (inv * inv * inv * mean)
        ).astype(BF16)
        pl.when(sec > 0)(lambda: pass_grad(m).start())
        if m < mbs - 1:
            scatter(m)

    for m in range(mbs):
        pl.loop(1, n)(lambda d: part_copy(m, d).wait_recv())
        rs_s[m, 0] = part_s[m, me]
        total = jnp.sum(rs_s[m], axis=0)
        ko_ref[m] = total[0:own_heads]
        vo_ref[m] = total[own_heads:2 * own_heads]
    for m in range(mbs):
        pl.loop(1, n)(lambda d: part_copy(m, d).wait_send())
        pl.when(sec > 0)(lambda: pass_grad(m).wait_send())
    pl.loop(1, n)(lambda d: header_copy(d).wait_send())
    for w in (0, 1):
        for k in range(line):
            for slot in slots_of(k):
                finish(w, slot)


def per_device(
    section_input,
    out_grad,
    norm_gain,
    query_weight,
    output_weight,
    header_keys,
    header_values,
    header_pos,
    segment_ids,
):
    sections = lax.axis_size("section")
    n = lax.axis_size("seq")
    mbs, rows, width = section_input.shape[1:]
    own_heads, kv_width = header_keys.shape[2:]
    heads = own_heads * n
    span = GROUP * heads
    qw = query_weight.shape[2]
    slots = 2 * (n // 4) - 1
    vmem = pl.BlockSpec(memory_space=pltpu.VMEM)
    dma = pltpu.SemaphoreType.DMA
    grads, keys, values = pl.pallas_call(
        functools.partial(kernel, n, sections),
        out_shape=(
            jax.ShapeDtypeStruct((mbs, rows, width), BF16),
            jax.ShapeDtypeStruct((mbs, own_heads, kv_width), F32),
            jax.ShapeDtypeStruct((mbs, own_heads, kv_width), F32),
        ),
        in_specs=[vmem] * 9,
        out_specs=[vmem] * 3,
        scratch_shapes=[
            pltpu.VMEM((width, qw), BF16),
            pltpu.VMEM((qw, width), BF16),
            pltpu.VMEM((n, 2 * mbs * own_heads, kv_width), F32),
            pltpu.VMEM((2 * mbs, heads, kv_width), F32),
            pltpu.VMEM((mbs, KEY_HEADS, span, LANES), BF16),
            pltpu.VMEM((mbs, KEY_HEADS, span, LANES), BF16),
            pltpu.VMEM((mbs * rows, width), BF16),
            pltpu.VMEM((mbs, rows, 128), F32),
            pltpu.VMEM((rows, LANES), F32),
            pltpu.VMEM((rows, LANES), F32),
            pltpu.VMEM((mbs, heads, LANES), F32),
            pltpu.VMEM((mbs, heads, LANES), F32),
            pltpu.VMEM((mbs, rows, qw), BF16),
            pltpu.VMEM((mbs, rows, KEY_HEADS * span), BF16),
            pltpu.VMEM((mbs, rows, width), BF16),
            pltpu.VMEM((rows, qw), BF16),
            pltpu.VMEM((rows, width), F32),
            pltpu.VMEM((2, heads, kv_width), F32),
            pltpu.VMEM((mbs, n, 2 * own_heads, kv_width), F32),
            pltpu.VMEM((mbs, n, 2 * own_heads, kv_width), F32),
            dma((2, 5, slots)),
            dma((2, 4, slots)),
            dma((n,)),
            dma((n,)),
            dma((mbs,)),
            dma((mbs,)),
            dma((mbs, n)),
            dma((mbs, n)),
        ],
        compiler_params=pltpu.CompilerParams(
            collective_id=0, has_side_effects=True, vmem_limit_bytes=56 << 20
        ),
        name="relay_backward",
    )(
        section_input[0], out_grad, norm_gain, query_weight[0], output_weight[0],
        header_keys[0], header_values[0], header_pos, segment_ids,
    )
    return (grads[None], keys[None], values[None])


def solution(mesh):
    in_specs = (
        P("section", None, "seq", None),
        P(None, "seq", None),
        P("section", None),
        P("section", "seq", None),
        P("section", "seq", None),
        P("section", None, "seq", None),
        P("section", None, "seq", None),
        P(),
        P(None, "seq"),
    )
    out_specs = (
        P("section", None, "seq", None),
        P("section", None, "seq", None),
        P("section", None, "seq", None),
    )
    return jax.shard_map(
        per_device, mesh=mesh, in_specs=in_specs, out_specs=out_specs, check_vma=False
    )
```

```python
import functools
import math

import jax
import jax.numpy as jnp
from jax import lax
from jax.experimental import pallas as pl
from jax.experimental.pallas import tpu as pltpu
from jax.sharding import PartitionSpec as P

KEY_HEADS = 4
HEAD_WIDTH = 64
HPS = 8
GROUP = 4
LANES = GROUP * HEAD_WIDTH

EPSILON = 1e-05
ROPE_BASE = 500000.0
MESH = pl.DeviceIdType.MESH
NT = (((1,), (1,)), ((), ()))
TN = (((0,), (0,)), ((), ()))
NN = (((1,), (0,)), ((), ()))
F32 = jnp.float32
BF16 = jnp.bfloat16


def mm(a, b, dims):
    return lax.dot_general(a, b, dims, preferred_element_type=F32)


def as_column(row):
    k = row.shape[1]
    same = lax.broadcasted_iota(jnp.int32, (k, k), 0) == lax.broadcasted_iota(jnp.int32, (k, k), 1)
    return jnp.sum(jnp.where(same, row, 0.0), axis=1, keepdims=True)


def rope_wide(positions):
    half = HEAD_WIDTH // 2
    lane = lax.broadcasted_iota(jnp.int32, (positions.shape[0], 128), 1)
    inverse = jnp.exp((lane % half).astype(F32) * (-2.0 * math.log(ROPE_BASE) / (2 * half)))
    angles = positions * inverse
    cosine, sine = jnp.cos(angles), jnp.sin(angles)
    sine = jnp.where(lane % HEAD_WIDTH < half, -sine, sine)
    return jnp.concatenate([cosine] * (LANES // 128), axis=1), jnp.concatenate([sine] * (LANES // 128), axis=1)


def half_swap(v):
    width = v.shape[1]
    half = HEAD_WIDTH // 2
    lane = lax.broadcasted_iota(jnp.int32, v.shape, 1)
    from_right = pltpu.roll(v, width - half, 1)
    from_left = pltpu.roll(v, half, 1)
    return jnp.where(lane % HEAD_WIDTH < half, from_right, from_left)


def rotate(v, cosine, signed_sine):
    return v * cosine + half_swap(v) * signed_sine


def fold_heads(v):
    v = v + pltpu.roll(v, 2 * HEAD_WIDTH, 1)
    return v + pltpu.roll(v, HEAD_WIDTH, 1)


def block_sum(v, ones_block):
    high = v.astype(BF16)
    low = (v - high.astype(F32)).astype(BF16)
    return mm(high, ones_block, NN) + mm(low, ones_block, NN)


def kernel(
    n, sections, *refs
):
    (
        x_ref, og_ref, gain_ref, wq_ref, wo_ref, hk_ref, hv_ref, pos_ref, seg_ref,
        gi_ref, ko_ref, vo_ref,
        wq_s, wo_s, hdr_s, hd_s, kb_s, vb_s, normed_s, inv_s, cos_s, sin_s, hcos_s, hsin_s, q_s, p_s, gin_s, gq_s, gn_s, acc_s, part_s, rs_s,
        ssem, rsem, hs_sem, hr_sem, gs_sem, gr_sem, rss_sem, rsr_sem,
    ) = refs
    me = lax.axis_index("seq")
    sec = lax.axis_index("section")
    mbs, rows, width = x_ref.shape
    heads = pos_ref.shape[1]
    own_heads = heads // n
    span = GROUP * heads
    line = n // 4
    a, b, c = me // 4, (me // 2) % 2, me % 2

    barrier = pltpu.get_barrier_semaphore()

    @pl.loop(1, n)
    def _(d):
        pl.semaphore_signal(barrier, inc=1, device_id={"seq": (me + d) % n}, device_id_type=MESH)

    @pl.when(sec > 0)
    def _():
        pl.semaphore_signal(barrier, inc=1, device_id={"section": sec - 1}, device_id_type=MESH)

    @pl.when(sec < sections - 1)
    def _():
        pl.semaphore_signal(barrier, inc=1, device_id={"section": sec + 1}, device_id_type=MESH)

    rq, ro = wq_ref.shape[0], wo_ref.shape[0]
    wq_s[pl.ds(pl.multiple_of(me * rq, rq), rq), :] = wq_ref[...]
    wo_s[pl.ds(pl.multiple_of(me * ro, ro), ro), :] = wo_ref[...]
    own_headers = [hk_ref[m].astype(F32) for m in range(mbs)] + [hv_ref[m].astype(F32) for m in range(mbs)]
    hdr_s[me] = jnp.concatenate(own_headers, axis=0)
    neighbours = (sec > 0).astype(jnp.int32) + (sec < sections - 1).astype(jnp.int32)
    pl.semaphore_wait(barrier, n - 1 + neighbours)

    def spot(aa, bb, cc):
        return aa * 4 + bb * 2 + cc

    def block(w, owner):
        scr, r = ((wq_s, rq), (wo_s, ro))[w]
        return scr.at[pl.ds(pl.multiple_of(owner * r, r), r), :]

    def copy(w, owner, send, recv, target):
        return pltpu.make_async_remote_copy(
            src_ref=block(w, owner),
            dst_ref=block(w, owner),
            send_sem=ssem.at[w, send[0], send[1]],
            recv_sem=rsem.at[w, recv[0], recv[1]],
            device_id={"seq": target},
            device_id_type=MESH,
        )

    def owner_line(slot):
        return a - slot if slot < line else a + (slot - line + 1)

    def valid(slot):
        if slot == 0:
            return a >= 0
        return (a >= slot) if slot < line else (a + (slot - line + 1) < line)

    def up(w, slot):
        return copy(w, spot(owner_line(slot), b, c), (0, slot), (0, slot + 1), spot(a + 1, b, c))

    def down(w, slot):
        later = line if slot == 0 else slot + 1
        return copy(w, spot(owner_line(slot), b, c), (1, slot), (0, later), spot(a - 1, b, c))

    def across(w, slot):
        return copy(w, spot(owner_line(slot), b, c), (2, slot), (1, slot), spot(a, 1 - b, c))

    def core_a(w, slot):
        return copy(w, spot(owner_line(slot), b, c), (3, slot), (2, slot), spot(a, b, 1 - c))

    def core_b(w, slot):
        return copy(w, spot(owner_line(slot), 1 - b, c), (4, slot), (3, slot), spot(a, b, 1 - c))

    def arrived(w, owner, kind, slot):
        copy(w, owner, (0, 0), (kind, slot), spot(a, b, 1 - c)).wait_recv()

    def goes_up(slot):
        return slot < line - 1

    def goes_down(slot):
        return slot == 0 or (line <= slot and slot < 2 * line - 2)

    def send_on(w, slot):
        if goes_up(slot):
            pl.when(valid(slot) & (a + 1 < line))(lambda: up(w, slot).start())
        if goes_down(slot):
            pl.when(valid(slot) & (a > 0))(lambda: down(w, slot).start())

        @pl.when(valid(slot))
        def _():
            across(w, slot).start()
            core_a(w, slot).start()

    def take_line(w, slot):
        pl.when(valid(slot))(lambda: arrived(w, spot(owner_line(slot), b, c), 0, slot))
        send_on(w, slot)

    def take_across(w, slot):
        @pl.when(valid(slot))
        def _():
            arrived(w, spot(owner_line(slot), 1 - b, c), 1, slot)
            core_b(w, slot).start()

    def take_core(w, slot):
        @pl.when(valid(slot))
        def _():
            arrived(w, spot(owner_line(slot), b, 1 - c), 2, slot)
            arrived(w, spot(owner_line(slot), 1 - b, 1 - c), 3, slot)

    def finish(w, slot):
        if goes_up(slot):
            pl.when(valid(slot) & (a + 1 < line))(lambda: up(w, slot).wait_send())
        if goes_down(slot):
            pl.when(valid(slot) & (a > 0))(lambda: down(w, slot).wait_send())

        @pl.when(valid(slot))
        def _():
            across(w, slot).wait_send()
            core_a(w, slot).wait_send()
            core_b(w, slot).wait_send()

    def slots_of(k):
        return [0] if k == 0 else [k, line - 1 + k]

    def header_copy(d):
        return pltpu.make_async_remote_copy(
            src_ref=hdr_s.at[me],
            dst_ref=hdr_s.at[me],
            send_sem=hs_sem.at[d],
            recv_sem=hr_sem.at[d],
            device_id={"seq": (me + d) % n},
            device_id_type=MESH,
        )

    def header_arrival(d):
        source = (me + n - d) % n
        return pltpu.make_async_remote_copy(
            src_ref=hdr_s.at[source],
            dst_ref=hdr_s.at[source],
            send_sem=hs_sem.at[d],
            recv_sem=hr_sem.at[d],
            device_id={"seq": (me + d) % n},
            device_id_type=MESH,
        )

    pl.loop(1, n)(lambda d: header_copy(d).start())
    for w in (0, 1):
        send_on(w, 0)

    lane = lax.broadcasted_iota(jnp.int32, (heads, LANES), 1) // HEAD_WIDTH

    def prepare_rows():
        for m in range(mbs):
            wide = x_ref[m].astype(F32)
            inv = lax.rsqrt(jnp.mean(wide * wide, axis=-1, keepdims=True) + EPSILON)
            inv_s[m] = jnp.broadcast_to(inv, (rows, 128))
            normed_s[m * rows:(m + 1) * rows, :] = (wide * inv * gain_ref[...]).astype(BF16)

        @pl.when(sec == sections - 1)
        def _():
            gin_s[...] = og_ref[...]

    def prepare_headers():
        cos_s[...], sin_s[...] = rope_wide(
            (me * rows + lax.broadcasted_iota(jnp.int32, (rows, 1), 0)).astype(F32)
        )
        for m in range(mbs):
            hcos_s[m], hsin_s[m] = rope_wide(as_column(pos_ref[m:m + 1, :].astype(F32)))

        pl.loop(1, n)(lambda d: header_arrival(d).wait_recv())
        for i in range(n):
            for j in range(2 * mbs):
                hd_s[j, i * own_heads:(i + 1) * own_heads, :] = hdr_s[i, j * own_heads:(j + 1) * own_heads, :]

        def spread(v, g):
            return fold_heads(jnp.where(lane == g, v, 0.0))

        for m in range(mbs):
            keys = rotate(hd_s[m], hcos_s[m], hsin_s[m]).astype(BF16).astype(F32)
            values = hd_s[mbs + m]
            for g in range(KEY_HEADS):
                wide_k, wide_v = spread(keys, g), spread(values, g)
                for j in range(GROUP):
                    kb_s[m, g, j * heads:(j + 1) * heads, :] = jnp.where(lane == j, wide_k, 0.0).astype(BF16)
                    vb_s[m, g, j * heads:(j + 1) * heads, :] = jnp.where(lane == j, wide_v, 0.0).astype(BF16)

    ones_block = (
        lax.broadcasted_iota(jnp.int32, (span, span), 0) // heads
        == lax.broadcasted_iota(jnp.int32, (span, span), 1) // heads
    ).astype(F32).astype(BF16)
    column = lax.broadcasted_iota(jnp.int32, (rows, span), 1)
    column_segment = (column % heads) // HPS
    segment_columns = [as_column(seg_ref[m:m + 1, :].astype(F32)).astype(jnp.int32) for m in range(mbs)]
    scale = HEAD_WIDTH ** (-0.5)

    def forward(g):
        cols = slice(g * LANES, (g + 1) * LANES)
        projected = mm(normed_s[...], wq_s[:, cols], NN)
        for m in range(mbs):
            query = rotate(projected[m * rows:(m + 1) * rows], cosine, sine).astype(BF16)
            q_s[m, :, cols] = query
            score = mm(query, kb_s[m, g], NT) * scale
            weight = jnp.where(segment_columns[m] == column_segment, jnp.exp(score), 0.0)
            p_s[m, :, g * span:(g + 1) * span] = (weight / block_sum(weight, ones_block)).astype(BF16)

    def relay(w, k):
        for slot in slots_of(k):
            take_line(w, slot)
        for slot in slots_of(k - 1):
            take_across(w, slot)

    def last_across(w):
        for slot in slots_of(line - 1):
            take_across(w, slot)

    def all_core(w):
        for k in range(line):
            for slot in slots_of(k):
                take_core(w, slot)

    prepare_rows()
    for k in range(1, line):
        relay(0, k)
        if k > 1:
            relay(1, k - 1)
        if k == 2:
            prepare_headers()
    last_across(0)
    all_core(0)
    cosine, sine = cos_s[...], sin_s[...]
    forward(0)
    relay(1, line - 1)
    forward(1)
    last_across(1)
    for g in range(2, KEY_HEADS):
        forward(g)
    all_core(1)

    diag = (
        lax.broadcasted_iota(jnp.int32, (span, LANES), 0) // heads
        == lax.broadcasted_iota(jnp.int32, (span, LANES), 1) // HEAD_WIDTH
    )

    def folded(product):
        kept = jnp.where(diag, product, 0.0)
        total = kept[0:heads]
        for j in range(1, GROUP):
            total = total + kept[j * heads:(j + 1) * heads]
        return fold_heads(total)

    def pass_grad(m):
        return pltpu.make_async_remote_copy(
            src_ref=gi_ref.at[m],
            dst_ref=gin_s.at[m],
            send_sem=gs_sem.at[m],
            recv_sem=gr_sem.at[m],
            device_id={"section": jnp.maximum(sec - 1, 0)},
            device_id_type=MESH,
        )

    def part_copy(m, d):
        return pltpu.make_async_remote_copy(
            src_ref=part_s.at[m, (me + d) % n],
            dst_ref=rs_s.at[m, d],
            send_sem=rss_sem.at[m, d],
            recv_sem=rsr_sem.at[m, d],
            device_id={"seq": (me + d) % n},
            device_id_type=MESH,
        )

    def scatter(m):
        key_total = rotate(acc_s[0], hcos_s[m], -hsin_s[m])
        value_total = acc_s[1]
        for i in range(n):
            part_s[m, i, 0:own_heads, :] = key_total[i * own_heads:(i + 1) * own_heads]
            part_s[m, i, own_heads:2 * own_heads, :] = value_total[i * own_heads:(i + 1) * own_heads]
        pl.loop(1, n)(lambda d: part_copy(m, d).start())

    tile = 256
    for m in range(mbs):
        pl.when(sec < sections - 1)(lambda: pass_grad(m).wait_recv())
        acc_s[...] = jnp.zeros_like(acc_s)

        for g in range(KEY_HEADS):
            cols = slice(g * LANES, (g + 1) * LANES)
            wide_cols = slice(g * span, (g + 1) * span)
            head_grad = mm(gin_s[m], wo_s[cols, :], NT).astype(BF16)
            probs = p_s[m, :, wide_cols]
            broad = probs.astype(F32)
            grad_probs = mm(head_grad, vb_s[m, g], NT)
            row_total = block_sum(broad * grad_probs, ones_block)
            grad_scores = (broad * (grad_probs - row_total) * scale).astype(BF16)
            grad_rot = mm(grad_scores, kb_s[m, g], NN)
            gq_s[:, cols] = rotate(grad_rot, cosine, -sine).astype(BF16)
            key_part = folded(mm(grad_scores, q_s[m, :, cols], TN))
            value_part = folded(mm(probs, head_grad, TN))
            here = lane == g
            acc_s[0] = jnp.where(here, key_part, acc_s[0])
            acc_s[1] = jnp.where(here, value_part, acc_s[1])

        if m == mbs - 1:
            scatter(m)

        for t in range(width // tile):
            cols = slice(t * tile, (t + 1) * tile)
            gn_s[:, cols] = mm(gq_s[...], wq_s[cols, :], NT) * gain_ref[:, cols]

        wide = x_ref[m].astype(F32)
        scaled = gn_s[...]
        inv = inv_s[m][:, 0:1]
        mean = jnp.mean(wide * scaled, axis=-1, keepdims=True)
        gi_ref[m] = (
            gin_s[m].astype(F32) + inv * scaled - wide * (inv * inv * inv * mean)
        ).astype(BF16)
        pl.when(sec > 0)(lambda: pass_grad(m).start())
        if m < mbs - 1:
            scatter(m)

    for m in range(mbs):
        pl.loop(1, n)(lambda d: part_copy(m, d).wait_recv())
        rs_s[m, 0] = part_s[m, me]
        total = jnp.sum(rs_s[m], axis=0)
        ko_ref[m] = total[0:own_heads]
        vo_ref[m] = total[own_heads:2 * own_heads]
    for m in range(mbs):
        pl.loop(1, n)(lambda d: part_copy(m, d).wait_send())
        pl.when(sec > 0)(lambda: pass_grad(m).wait_send())
    pl.loop(1, n)(lambda d: header_copy(d).wait_send())
    for w in (0, 1):
        for k in range(line):
            for slot in slots_of(k):
                finish(w, slot)


def per_device(
    section_input,
    out_grad,
    norm_gain,
    query_weight,
    output_weight,
    header_keys,
    header_values,
    header_pos,
    segment_ids,
):
    sections = lax.axis_size("section")
    n = lax.axis_size("seq")
    mbs, rows, width = section_input.shape[1:]
    own_heads, kv_width = header_keys.shape[2:]
    heads = own_heads * n
    span = GROUP * heads
    qw = query_weight.shape[2]
    slots = 2 * (n // 4) - 1
    vmem = pl.BlockSpec(memory_space=pltpu.VMEM)
    dma = pltpu.SemaphoreType.DMA
    grads, keys, values = pl.pallas_call(
        functools.partial(kernel, n, sections),
        out_shape=(
            jax.ShapeDtypeStruct((mbs, rows, width), BF16),
            jax.ShapeDtypeStruct((mbs, own_heads, kv_width), F32),
            jax.ShapeDtypeStruct((mbs, own_heads, kv_width), F32),
        ),
        in_specs=[vmem] * 9,
        out_specs=[vmem] * 3,
        scratch_shapes=[
            pltpu.VMEM((width, qw), BF16),
            pltpu.VMEM((qw, width), BF16),
            pltpu.VMEM((n, 2 * mbs * own_heads, kv_width), F32),
            pltpu.VMEM((2 * mbs, heads, kv_width), F32),
            pltpu.VMEM((mbs, KEY_HEADS, span, LANES), BF16),
            pltpu.VMEM((mbs, KEY_HEADS, span, LANES), BF16),
            pltpu.VMEM((mbs * rows, width), BF16),
            pltpu.VMEM((mbs, rows, 128), F32),
            pltpu.VMEM((rows, LANES), F32),
            pltpu.VMEM((rows, LANES), F32),
            pltpu.VMEM((mbs, heads, LANES), F32),
            pltpu.VMEM((mbs, heads, LANES), F32),
            pltpu.VMEM((mbs, rows, qw), BF16),
            pltpu.VMEM((mbs, rows, KEY_HEADS * span), BF16),
            pltpu.VMEM((mbs, rows, width), BF16),
            pltpu.VMEM((rows, qw), BF16),
            pltpu.VMEM((rows, width), F32),
            pltpu.VMEM((2, heads, kv_width), F32),
            pltpu.VMEM((mbs, n, 2 * own_heads, kv_width), F32),
            pltpu.VMEM((mbs, n, 2 * own_heads, kv_width), F32),
            dma((2, 5, slots)),
            dma((2, 4, slots)),
            dma((n,)),
            dma((n,)),
            dma((mbs,)),
            dma((mbs,)),
            dma((mbs, n)),
            dma((mbs, n)),
        ],
        compiler_params=pltpu.CompilerParams(
            collective_id=0, has_side_effects=True, vmem_limit_bytes=56 << 20
        ),
        name="relay_backward",
    )(
        section_input[0], out_grad, norm_gain, query_weight[0], output_weight[0],
        header_keys[0], header_values[0], header_pos, segment_ids,
    )
    return (grads[None], keys[None], values[None])


def solution(mesh):
    in_specs = (
        P("section", None, "seq", None),
        P(None, "seq", None),
        P("section", None),
        P("section", "seq", None),
        P("section", "seq", None),
        P("section", None, "seq", None),
        P("section", None, "seq", None),
        P(),
        P(None, "seq"),
    )
    out_specs = (
        P("section", None, "seq", None),
        P("section", None, "seq", None),
        P("section", None, "seq", None),
    )
    return jax.shard_map(
        per_device, mesh=mesh, in_specs=in_specs, out_specs=out_specs, check_vma=False
    )
```
